512 devices in a mesh: dp: 32 (over x, y, core), mp: 16 (over z).
Axes of the slice: x: 4, y: 4, z: 16, core: 2. Of those that a mesh axis runs over, the one named last changes fastest.
Arguments:
- hidden: bfloat16 [65536, 4096], P('dp', 'mp'), may hold values from -600 to 600
- segments: int32 [512, 128], P('dp'), may hold values from 0 to 5, never falling along the last dimension, each value on 1 to 40 neighbouring positions
- counts: int32 [32], replicated, may hold values from 1 to 16, 256 in all
- dest_order: int32 [32], replicated, may hold values from 0 to 31, each once
- norm_gain: bfloat16 [4096], replicated, may hold values from 0.5 to 1.5
- q_weight: bfloat16 [4096, 4096], P(None, 'mp'), may hold values from -1.921875 to 1.921875
- kv_weight: bfloat16 [4096, 2048], P(None, 'mp'), may hold values from -0.09375 to 0.09375
Outputs:
- attended: bfloat16 [32768, 4096], P('dp', 'mp')
The draws below stay inside these ranges and needn't reach their ends.
Inputs may be any that keep to these rules, and one draw needn't show every extreme that they name: counts sum to 256 and reach 16 on some index of dp. `segments`: ids never fall within a block; a hypothesis spans at most 40 tokens.
All inputs are finite; a program needn't handle non-finite values.
Results may differ from the reference program's by a relative error of at most 0.0073.
Values may be sent and summed in bfloat16 or wider, within the bound.
A program may use at most 64 MiB of HBM per device.

```python
import math
import jax
import jax.numpy as jnp
import numpy as np
from jax import lax

D = 4096
HQ = 32
KV = 8
HD = 128
BLOCK = 128
KEEP = 8
SLOTS = 16
SHARE = 2
BLOCKS = 512
ROWS = 65536
N_DP = 32


def weight_bases(key):
    scale = D ** (-0.5)
    key_part = jnp.clip(jax.random.normal(jax.random.fold_in(key, 11), (D, KV, HD), jnp.float32), -6.0, 6.0) * scale
    value_part = jnp.clip(jax.random.normal(jax.random.fold_in(key, 12), (D, KV, HD), jnp.float32), -6.0, 6.0) * scale
    return (key_part, value_part)


def draw_hidden(key, part):
    columns = 10.0 ** (jnp.arange(D, dtype=jnp.float32) / D)
    scales = 10.0 ** jax.random.uniform(jax.random.fold_in(key, 22), (ROWS, 1), jnp.float32)
    base = jnp.clip(jax.random.normal(jax.random.fold_in(key, 21), (ROWS, D), jnp.float32), -6.0, 6.0)
    return (base * columns[None, :] * scales).astype(jnp.bfloat16)


def draw_q_weight(key, part):
    noise = jnp.clip(jax.random.normal(jax.random.fold_in(key, 13), (D, HQ, HD), jnp.float32), -6.0, 6.0) * D ** (-0.5)
    result = noise
    return result.reshape(D, HQ * HD).astype(jnp.bfloat16)


def draw_kv_weight(key, part):
    key_part, value_part = weight_bases(key)
    piece = HD // SHARE
    stacked = jnp.stack([key_part.reshape(D, KV, SHARE, piece), value_part.reshape(D, KV, SHARE, piece)], axis=3)
    return stacked.reshape(D, 2 * KV * HD).astype(jnp.bfloat16)


def split_up(count, total, most, slope):
    portions = [(1 << 20) // math.isqrt(grade ** slope) + 1 for grade in range(2, count + 1)]
    rest, given = total - most - (count - 1), [1] * (count - 1)
    while rest > 0:
        free = [i for i in range(count - 1) if given[i] < most]
        pool, budget = sum([portions[i] for i in free]), rest
        for i in free:
            more = min(most - given[i], max(1, budget * portions[i] // pool), rest)
            given[i] = given[i] + more
            rest = rest - more
    return np.array([most] + given)


def ragged(own_key, number_of, total, reach, lean):
    if number_of == 2:
        one = jax.random.randint(own_key, (), max(1, total - reach), min(reach, total - 1) + 1)
        return jnp.stack([one, total - one])
    sizes = jnp.asarray(split_up(number_of, total, reach, lean), jnp.int32)
    twos = (number_of - 1) // 2
    source_of, receiver = sizes[1:1 + 2 * twos:2], sizes[2:2 + 2 * twos:2]
    margin = jnp.minimum(source_of - 1, reach - receiver)
    moved = jax.random.randint(jax.random.fold_in(own_key, 1), (twos,), 0, 1 << 20) % (margin + 1)
    sizes = sizes.at[1:1 + 2 * twos:2].set(source_of - moved).at[2:2 + 2 * twos:2].set(receiver + moved)
    return sizes[jax.random.permutation(jax.random.fold_in(own_key, 2), number_of)]


def setup_inputs(seed: int = 0) -> dict:
    keys = jax.random.split(jax.random.key(seed), 8)
    return {
        "hidden": draw_hidden(jax.random.fold_in(keys[7], 71), 0),
        "segments": jax.vmap(lambda own: jnp.searchsorted(jnp.cumsum(ragged(own, 6, BLOCK, 40, 0)), jnp.arange(BLOCK), side="right"))(jax.random.split(keys[1], BLOCKS)).reshape((BLOCKS, BLOCK)).astype(jnp.int32),
        "counts": ragged(keys[2], N_DP, N_DP * KEEP, SLOTS, 2).astype(jnp.int32),
        "dest_order": jax.random.permutation(keys[3], N_DP).astype(jnp.int32),
        "norm_gain": jnp.clip(1.0 + 0.1 * jax.random.normal(keys[4], (D,), jnp.float32), 0.5, 1.5).astype(jnp.bfloat16),
        "q_weight": draw_q_weight(jax.random.fold_in(keys[7], 71), 0),
        "kv_weight": draw_kv_weight(jax.random.fold_in(keys[7], 71), 0),
    }


epsilon = 1e-05
rope_base = 500000.0

def rope_tables(positions, width):
    halves = width // 2
    frequency = rope_base ** (-(jnp.arange(halves, dtype=jnp.float32) * 2.0) / width)
    angles = positions.astype(jnp.float32)[..., None] * frequency
    return (jnp.cos(angles), jnp.sin(angles))

def rotate(tensor, cosine, sine_part):
    halves = tensor.shape[-1] // 2
    lower = tensor[..., :halves]
    upper = tensor[..., halves:]
    cosine = cosine[..., None, :]
    sine_part = sine_part[..., None, :]
    return jnp.concatenate([lower * cosine - upper * sine_part, upper * cosine + lower * sine_part], axis=-1)

def segment_masks(block_segments):
    length = block_segments.shape[-1]
    column = jnp.arange(length, dtype=jnp.int32)
    same_segment = block_segments[:, :, None] == block_segments[:, None, :]
    before = column[None, :] < column[:, None]
    positions = lax.optimization_barrier(jnp.sum((same_segment & before[None]).astype(jnp.int32), axis=2))
    visible = same_segment & (column[None, :] <= column[:, None])[None]
    return (positions, visible)

def attend(rows, block_segments, norm_gain, q_weight, k_weight, v_weight):
    count_blocks = block_segments.shape[0]
    block_len = block_segments.shape[1]
    widened = rows.astype(jnp.float32)
    row_scale = lax.rsqrt(lax.optimization_barrier(jnp.mean(widened * widened, axis=1, keepdims=True)) + epsilon)
    normed = (widened * norm_gain.astype(jnp.float32)).astype(jnp.bfloat16)
    queries = row_scale * jnp.dot(normed, q_weight, preferred_element_type=jnp.float32)
    key_raw = (row_scale * jnp.dot(normed, k_weight, preferred_element_type=jnp.float32)).astype(jnp.bfloat16)
    value_rows = (row_scale * jnp.dot(normed, v_weight, preferred_element_type=jnp.float32)).astype(jnp.bfloat16)
    positions, visible = segment_masks(block_segments)
    cosine, sine_part = rope_tables(positions, HD)
    query_rows = rotate(queries.reshape(count_blocks, block_len, HQ, HD), cosine, sine_part).astype(jnp.bfloat16)
    key_rows = rotate(key_raw.astype(jnp.float32).reshape(count_blocks, block_len, KV, HD), cosine, sine_part).astype(jnp.bfloat16)
    values = value_rows.reshape(count_blocks, block_len, KV, HD)
    grouped = query_rows.reshape(count_blocks, block_len, KV, HQ // KV, HD)
    scores = jnp.einsum('nikgd,njkd->nkgij', grouped.astype(jnp.float32), key_rows.astype(jnp.float32)) * HD ** (-0.5)
    scores = jnp.where(visible[:, None, None], scores, -jnp.inf)
    highest = lax.optimization_barrier(jnp.max(scores, axis=-1, keepdims=True))
    weights = jnp.exp(scores - highest)
    shares = (weights / lax.optimization_barrier(jnp.sum(weights, axis=-1, keepdims=True))).astype(jnp.bfloat16)
    mixture = jnp.einsum('nkgij,njkd->nikgd', shares.astype(jnp.float32), values.astype(jnp.float32))
    return mixture.reshape(count_blocks * block_len, HQ * HD).astype(jnp.bfloat16)

def reference(hidden, segments, counts, dest_order, norm_gain, q_weight, kv_weight):
    device_ids = jnp.arange(N_DP, dtype=jnp.int32)
    starts = (jnp.cumsum(counts) - counts).astype(jnp.int32)
    finishes = (starts + counts).astype(jnp.int32)
    position_of = lax.optimization_barrier(jnp.sum(device_ids[None, :] * (dest_order[None, :] == device_ids[:, None]).astype(jnp.int32), axis=1)).astype(jnp.int32)
    global_ids = (jnp.arange(KEEP, dtype=jnp.int32)[None, :] * N_DP + position_of[:, None]).astype(jnp.int32)
    sources = lax.optimization_barrier(jnp.sum((finishes[None, None, :] <= global_ids[:, :, None]).astype(jnp.int32), axis=2)).astype(jnp.int32)
    picked = (sources * SLOTS + global_ids - starts[sources]).reshape(-1).astype(jnp.int32)
    blocks = hidden.reshape(BLOCKS, BLOCK, D)[picked].reshape(N_DP, KEEP * BLOCK, D)
    block_segments = segments[picked].reshape(N_DP, KEEP, BLOCK)
    kv_split = kv_weight.reshape(D, KV, SHARE, 2, HD // SHARE)
    k_weight = kv_split[:, :, :, 0, :].reshape(D, KV * HD)
    v_weight = kv_split[:, :, :, 1, :].reshape(D, KV * HD)

    def one_device(inputs):
        return attend(inputs[0], inputs[1], norm_gain, q_weight, k_weight, v_weight)
    outputs = lax.map(one_device, (blocks, block_segments))
    return outputs.reshape(N_DP * KEEP * BLOCK, HQ * HD)
```

```python
import functools

import jax
import jax.numpy as jnp
import numpy as np
from jax import lax
from jax.experimental import pallas as pl
from jax.experimental.pallas import tpu as pltpu
from jax.sharding import PartitionSpec as P

HD = 128
HALF = HD // 2
GROUPS = 4
epsilon = 1e-05
rope_base = 500000.0
MASKED = -1e30
MESH = pl.DeviceIdType.MESH
f32 = jnp.float32
bf16 = jnp.bfloat16


def rope_table(length):
    frequency = rope_base ** (-(np.arange(HALF, dtype=np.float32) * 2.0) / HD)
    angles = np.arange(length, dtype=np.float32)[:, None] * frequency.astype(np.float32)
    cosine, sine = np.cos(angles), np.sin(angles)
    return np.concatenate([cosine, cosine, -sine, sine], axis=1).astype(np.float32)


def kernel(
    n_dp, n_mp, hidden, segments, counts, dest, gain, q_weight, kv_weight, table, out,
    hid, seg, wq, wkv, send, seg_send, seg_recv, recv0, recv1, recv2, recv3,
    ag, acc, squares, kv_mine, kv_theirs, q_rot, keys, values, tables, masks, gains, slots, sources,
    local_sem, send_sem, move_sem, seg_sem, ring_send, ring_recv, kv_send, kv_recv,
):
    recvs = (recv0, recv1, recv2, recv3)
    me_d = lax.axis_index("dp")
    me_z = lax.axis_index("mp")
    in_slots, block_len, width = hid.shape
    kept = in_slots // 2
    rows = block_len // GROUPS
    group_rows = kept * rows
    piece = group_rows // 2
    far = n_mp // 2
    near = far // 2
    right = lax.rem(me_z + 1, n_mp)
    left = lax.rem(me_z + n_mp - 1, n_mp)
    odd = lax.rem(me_z, 2)
    partner = me_z + 1 - 2 * odd

    local = [
        pltpu.make_async_copy(hidden, hid, local_sem.at[0]),
        pltpu.make_async_copy(segments, seg, local_sem.at[1]),
        pltpu.make_async_copy(q_weight, wq, local_sem.at[2]),
        pltpu.make_async_copy(kv_weight, wkv, local_sem.at[3]),
    ]
    for copy in local:
        copy.start()

    barrier = pltpu.get_barrier_semaphore()

    @pl.loop(1, n_dp)
    def _(offset):
        peer = lax.rem(me_d + offset, n_dp)
        pl.semaphore_signal(barrier, inc=1, device_id={"dp": peer}, device_id_type=MESH)

    for neighbour in (left, right):
        pl.semaphore_signal(barrier, inc=1, device_id={"mp": neighbour}, device_id_type=MESH)

    start = jnp.int32(0)
    for i in range(n_dp):
        start = start + jnp.where(i < me_d, counts[i], 0)
    count = counts[me_d]
    wanted = [
        jnp.where(s < count, dest[lax.rem(start + s, n_dp)], -1) for s in range(in_slots)
    ]

    @pl.loop(0, n_dp)
    def _(d):
        slot = jnp.int32(0)
        for s in range(1, in_slots):
            slot = slot + jnp.where(wanted[s] == d, s, 0)
        slots[d] = jnp.minimum(slot, in_slots - 1)

    local[0].wait()
    local[1].wait()

    def pack(g):
        @pl.loop(0, n_dp, unroll=4)
        def _(d):
            send[d, g * rows : (g + 1) * rows, :] = hid[slots[d], g * rows : (g + 1) * rows, :]

        recvs[g][me_d] = send[me_d, g * rows : (g + 1) * rows, :]

    def dispatch(g):
        @pl.loop(1, n_dp)
        def _(offset):
            peer = lax.rem(me_d + offset, n_dp)
            pltpu.make_async_remote_copy(
                send.at[peer, pl.ds(g * rows, rows)], recvs[g].at[me_d], send_sem.at[g], move_sem.at[g],
                device_id={"dp": peer}, device_id_type=MESH,
            ).start()

    pack(0)

    @pl.loop(0, n_dp)
    def _(d):
        seg_send[d] = seg[pl.ds(slots[d], 1), :]

    seg_recv[me_d] = seg_send[me_d]
    pl.semaphore_wait(barrier, n_dp + 1)
    dispatch(0)

    @pl.loop(1, n_dp)
    def _(offset):
        peer = lax.rem(me_d + offset, n_dp)
        pltpu.make_async_remote_copy(
            seg_send.at[peer], seg_recv.at[me_d], seg_sem.at[0], seg_sem.at[1],
            device_id={"dp": peer}, device_id_type=MESH,
        ).start()

    for g in range(1, GROUPS):
        pack(g)
        dispatch(g)

    mine = jnp.int32(0)
    for j in range(n_dp):
        mine = mine + jnp.where(dest[j] == me_d, j, 0)
    finish = jnp.int32(0)
    owners = [jnp.int32(0)] * kept
    for i in range(n_dp):
        finish = finish + counts[i]
        owners = [o + jnp.where(finish <= k * n_dp + mine, 1, 0) for k, o in enumerate(owners)]
    for k in range(kept):
        sources[k] = jnp.minimum(owners[k], n_dp - 1)

    gains[...] = gain[...].astype(f32)
    keys[...] = jnp.zeros_like(keys)
    values[...] = jnp.zeros_like(values)

    def ring_copy(z, g, p, s, way):
        block = ag.at[z, g, pl.ds(p * piece, piece)]
        return pltpu.make_async_remote_copy(
            block, block, ring_send.at[way, g], ring_recv.at[way, g, s - 1, p],
            device_id={"mp": right if way == 0 else left}, device_id_type=MESH,
        )

    def project(z, g, first=False):
        a = lax.rem(g, 2)
        x = ag[z, g].astype(f32)
        normed = (x * gains[pl.ds(z, 1), :]).astype(bf16)
        at = pl.ds(pl.multiple_of(z * width, width), width)
        queries = jnp.dot(normed, wq[at, :], preferred_element_type=f32)
        pieces = jnp.dot(normed, wkv[at, :], preferred_element_type=f32)
        sums = x[:, :HD] * x[:, :HD]
        for c in range(HD, width, HD):
            sums = sums + x[:, c : c + HD] * x[:, c : c + HD]
        if first:
            acc[a, :, : 2 * HD] = queries
            acc[a, :, 2 * HD :] = pieces
            squares[a] = sums
        else:
            acc[a, :, : 2 * HD] += queries
            acc[a, :, 2 * HD :] += pieces
            squares[a] += sums

    def open_group(g):
        pltpu.make_async_copy(
            recvs[g].at[pl.ds(0, n_dp - 1)], recvs[g].at[pl.ds(0, n_dp - 1)], move_sem.at[g]
        ).wait()
        for k in range(kept):
            ag[me_z, g, k * rows : (k + 1) * rows, :] = recvs[g][sources[k]]
        for p in range(2):
            for way in range(2):
                ring_copy(me_z, g, p, 1, way).start()
        if g == 0:
            local[2].wait()
            local[3].wait()

    def ring_step(g, s, late):
        from_left = lax.rem(me_z + n_mp - s, n_mp)
        from_right = lax.rem(me_z + s, n_mp)

        def arrive(p, way):
            z = from_left if way == 0 else from_right
            ring_copy(z, g, p, s, way).wait_recv()

        def forward(p, way):
            z = from_left if way == 0 else from_right
            ring_copy(z, g, p, s + 1, way).start()

        def both(p, way):
            arrive(p, way)
            forward(p, way)

        if not late:
            for p, way in ((0, 0), (1, 1), (1, 0), (0, 1)):
                both(p, way)
        else:
            for p, way in ((0, 0), (1, 1)):
                arrive(p, way)

                @pl.when(s < far)
                def _():
                    forward(p, way)

            @pl.when(s < far)
            def _():
                for p, way in ((1, 0), (0, 1)):
                    arrive(p, way)

                    @pl.when(s < far - 1)
                    def _():
                        forward(p, way)

        project(from_left, g)
        if not late:
            project(from_right, g)
        else:

            @pl.when(s < far)
            def _():
                project(from_right, g)

    def kv_copy(g):
        return pltpu.make_async_remote_copy(
            kv_mine.at[g], kv_theirs.at[g], kv_send.at[g], kv_recv.at[g],
            device_id={"mp": partner}, device_id_type=MESH,
        )

    def rotated(tensor, g):
        return (
            tensor * tables[g, :, :HD] + pltpu.roll(tensor, HALF, 1) * tables[g, :, HD:]
        ).astype(bf16)

    def close_group(g):
        a = lax.rem(g, 2)
        total = jnp.sum(squares[a], axis=1, keepdims=True)
        scale = lax.rsqrt(total / (n_mp * width) + epsilon)
        kv_mine[g] = (scale * acc[a, :, 2 * HD :]).astype(bf16)
        for h in range(2):
            q_rot[h] = rotated(scale * acc[a, :, h * HD : (h + 1) * HD], g)
        kv_copy(g).start()

    def attend(g):
        kv_copy(g).wait_recv()
        own = kv_mine[g].astype(f32)
        other = kv_theirs[g].astype(f32)
        upper = odd == 1
        leading = jnp.where(upper, other, own)
        trailing = jnp.where(upper, own, other)
        low = lax.broadcasted_iota(jnp.int32, own.shape, 1) < HALF
        key_raw = jnp.where(low, leading, pltpu.roll(trailing, HALF, 1))
        value = jnp.where(low, pltpu.roll(leading, HALF, 1), trailing).astype(bf16)
        key = rotated(key_raw, g)
        at = pl.ds(pl.multiple_of(g * rows, rows), rows)
        for k in range(kept):
            part = slice(k * rows, (k + 1) * rows)
            keys[k, at, :] = key[part]
            values[k, at, :] = value[part]
        for k in range(kept):
            part = slice(k * rows, (k + 1) * rows)
            query = jnp.concatenate([q_rot[0, part], q_rot[1, part]], axis=0)
            scores = lax.dot_general(
                query, keys[k], (((1,), (1,)), ((), ())), preferred_element_type=f32
            ) * HD ** (-0.5)
            visible = masks[g, part]
            visible = jnp.concatenate([visible, visible], axis=0)
            scores = jnp.where(visible > 0.5, scores, MASKED)
            weights = jnp.exp(scores - jnp.max(scores, axis=1, keepdims=True))
            shares = (weights / jnp.sum(weights, axis=1, keepdims=True)).astype(bf16)
            mixture = jnp.dot(shares, values[k], preferred_element_type=f32).astype(bf16)
            out[k, at, :HD] = mixture[:rows]
            out[k, at, HD:] = mixture[rows:]

    def prepare():
        pltpu.make_async_copy(
            seg_recv.at[pl.ds(0, n_dp - 1)], seg_recv.at[pl.ds(0, n_dp - 1)], seg_sem.at[1]
        ).wait()
        shape = (block_len, block_len)
        i = lax.broadcasted_iota(jnp.int32, shape, 0)
        j = lax.broadcasted_iota(jnp.int32, shape, 1)
        for k in range(kept):
            across = jnp.broadcast_to(seg_recv[sources[k]].astype(f32), shape)
            same = across == across.T
            position = jnp.sum(jnp.where(same & (j < i), 1.0, 0.0), axis=1, keepdims=True)
            visible = jnp.where(same & (j <= i), 1.0, 0.0)
            chosen = jnp.where(j.astype(f32) == position, 1.0, 0.0)
            turned = jnp.dot(
                chosen, table[...], precision=lax.Precision.HIGHEST, preferred_element_type=f32
            )
            for g in range(GROUPS):
                tables[g, k * rows : (k + 1) * rows, :] = turned[g * rows : (g + 1) * rows]
                masks[g, k * rows : (k + 1) * rows, :] = visible[g * rows : (g + 1) * rows]

    @pl.loop(0, GROUPS + 1)
    def _(turn):
        for g in range(GROUPS):

            @pl.when(turn == g)
            def _():
                open_group(g)

        @pl.when(turn < GROUPS)
        def _():
            project(me_z, turn, first=True)

        @pl.loop(1, near + 1)
        def _(s):
            @pl.when(turn > 0)
            def _():
                ring_step(turn - 1, s + near, True)

            @pl.when(turn < GROUPS)
            def _():
                ring_step(turn, s, False)

            @pl.when((s == 1) & (turn == 0))
            def _():
                prepare()

            @pl.when((s == near) & (turn > 1))
            def _():
                attend(turn - 2)

        @pl.when(turn > 0)
        def _():
            close_group(turn - 1)

    attend(GROUPS - 1)

    for g in range(GROUPS):
        moved = send.at[pl.ds(0, n_dp - 1), pl.ds(0, rows)]
        pltpu.make_async_copy(moved, moved, send_sem.at[g]).wait()
        passed = ag.at[pl.ds(0, n_mp - 1), 0, pl.ds(0, piece)]
        for way in range(2):
            pltpu.make_async_copy(passed, passed, ring_send.at[way, g]).wait()
        kv_copy(g).wait_send()
    pltpu.make_async_copy(
        seg_send.at[pl.ds(0, n_dp - 1)], seg_send.at[pl.ds(0, n_dp - 1)], seg_sem.at[0]
    ).wait()


def on_device(n_dp, n_mp, hidden, segments, counts, dest_order, norm_gain, q_weight, kv_weight):
    in_slots, block_len = segments.shape
    width = hidden.shape[1]
    kept = in_slots // 2
    rows = block_len // GROUPS
    group_rows = kept * rows
    depth = q_weight.shape[0]
    vmem, smem = (pl.BlockSpec(memory_space=space) for space in (pltpu.VMEM, pltpu.SMEM))
    anywhere = pl.BlockSpec(memory_space=pl.ANY)
    dma = pltpu.SemaphoreType.DMA
    result = pl.pallas_call(
        functools.partial(kernel, n_dp, n_mp),
        out_shape=jax.ShapeDtypeStruct((kept, block_len, width), bf16),
        in_specs=[anywhere, anywhere, smem, smem, vmem, anywhere, anywhere, vmem],
        out_specs=vmem,
        scratch_shapes=[
            pltpu.VMEM((in_slots, block_len, width), bf16),
            pltpu.VMEM((in_slots, block_len), jnp.int32),
            pltpu.VMEM((depth, 2 * HD), bf16),
            pltpu.VMEM((depth, HD), bf16),
            pltpu.VMEM((n_dp, block_len, width), bf16),
            pltpu.VMEM((n_dp, 1, block_len), jnp.int32),
            pltpu.VMEM((n_dp, 1, block_len), jnp.int32),
            *[pltpu.VMEM((n_dp, rows, width), bf16)] * GROUPS,
            pltpu.VMEM((n_mp, GROUPS, group_rows, width), bf16),
            pltpu.VMEM((2, group_rows, 3 * HD), f32),
            pltpu.VMEM((2, group_rows, HD), f32),
            pltpu.VMEM((GROUPS, group_rows, HD), bf16),
            pltpu.VMEM((GROUPS, group_rows, HD), bf16),
            pltpu.VMEM((2, group_rows, HD), bf16),
            pltpu.VMEM((kept, block_len, HD), bf16),
            pltpu.VMEM((kept, block_len, HD), bf16),
            pltpu.VMEM((GROUPS, group_rows, 2 * HD), f32),
            pltpu.VMEM((GROUPS, group_rows, HD), f32),
            pltpu.VMEM((n_mp, width), f32),
            pltpu.SMEM((n_dp,), jnp.int32),
            pltpu.SMEM((kept,), jnp.int32),
            dma((4,)),
            dma((GROUPS,)),
            dma((GROUPS,)),
            dma((2,)),
            dma((2, GROUPS)),
            dma((2, GROUPS, n_mp // 2, 2)),
            dma((GROUPS,)),
            dma((GROUPS,)),
        ],
        compiler_params=pltpu.CompilerParams(
            collective_id=0, has_side_effects=True, vmem_limit_bytes=60 * 1024 * 1024
        ),
        name="move_gather_attend",
    )(
        hidden.reshape(in_slots, block_len, width),
        segments,
        counts,
        dest_order,
        norm_gain.reshape(n_mp, width),
        q_weight,
        kv_weight,
        jnp.asarray(rope_table(block_len)),
    )
    return result.reshape(kept * block_len, width)


def solution(mesh):
    in_specs = (P("dp", "mp"), P("dp", None), P(), P(), P(), P(None, "mp"), P(None, "mp"))
    return jax.shard_map(
        functools.partial(on_device, mesh.shape["dp"], mesh.shape["mp"]),
        mesh=mesh,
        in_specs=in_specs,
        out_specs=P("dp", "mp"),
        check_vma=False,
    )
```

```python
import functools

import jax
import jax.numpy as jnp
import numpy as np
from jax import lax
from jax.experimental import pallas as pl
from jax.experimental.pallas import tpu as pltpu
from jax.sharding import PartitionSpec as P

HD = 128
HALF = HD // 2
GROUPS = 4
LAG = 1
epsilon = 1e-05
rope_base = 500000.0
MASKED = -1e30
MESH = pl.DeviceIdType.MESH
f32 = jnp.float32
bf16 = jnp.bfloat16


def rope_table(length):
    frequency = rope_base ** (-(np.arange(HALF, dtype=np.float32) * 2.0) / HD)
    angles = np.arange(length, dtype=np.float32)[:, None] * frequency.astype(np.float32)
    cosine, sine = np.cos(angles), np.sin(angles)
    return np.concatenate([cosine, cosine, -sine, sine], axis=1).astype(np.float32)


def kernel(n_dp, n_mp, hidden, segments, counts, dest, gain, q_weight, kv_weight, table, out, *scratch):
    hid, seg, wq, wkv, send, seg_send, seg_recv, *recvs = scratch[: 7 + GROUPS]
    (
        ag, acc, squares, kv_mine, kv_theirs, q_rot, keys, values, tables, masks, gains, done, slots, sources,
        local_sem, send_sem, move_sem, seg_sem, ring_send, ring_recv, kv_send, kv_recv, out_sem,
    ) = scratch[7 + GROUPS :]
    me_d = lax.axis_index("dp")
    me_z = lax.axis_index("mp")
    in_slots, block_len, width = hid.shape
    kept = in_slots // 2
    rows = block_len // GROUPS
    group_rows = kept * rows
    half = group_rows // 2
    far = n_mp // 2
    right = lax.rem(me_z + 1, n_mp)
    left = lax.rem(me_z + n_mp - 1, n_mp)
    odd = lax.rem(me_z, 2)
    partner = me_z + 1 - 2 * odd

    local = [
        pltpu.make_async_copy(hidden, hid, local_sem.at[0]),
        pltpu.make_async_copy(segments, seg, local_sem.at[1]),
        pltpu.make_async_copy(q_weight, wq, local_sem.at[2]),
        pltpu.make_async_copy(kv_weight, wkv, local_sem.at[3]),
    ]
    for copy in local:
        copy.start()

    barrier = pltpu.get_barrier_semaphore()

    @pl.loop(1, n_dp)
    def _(offset):
        peer = lax.rem(me_d + offset, n_dp)
        pl.semaphore_signal(barrier, inc=1, device_id={"dp": peer}, device_id_type=MESH)

    for neighbour in (left, right):
        pl.semaphore_signal(barrier, inc=1, device_id={"mp": neighbour}, device_id_type=MESH)

    start = jnp.int32(0)
    for i in range(n_dp):
        start = start + jnp.where(i < me_d, counts[i], 0)
    count = counts[me_d]
    wanted = [
        jnp.where(s < count, dest[lax.rem(start + s, n_dp)], -1) for s in range(in_slots)
    ]

    @pl.loop(0, n_dp)
    def _(d):
        slot = jnp.int32(0)
        for s in range(1, in_slots):
            slot = slot + jnp.where(wanted[s] == d, s, 0)
        slots[d] = jnp.minimum(slot, in_slots - 1)

    local[0].wait()
    local[1].wait()

    def pack(g):
        @pl.loop(0, n_dp, unroll=4)
        def _(d):
            send[d, g * rows : (g + 1) * rows, :] = hid[slots[d], g * rows : (g + 1) * rows, :]

        recvs[g][me_d] = send[me_d, g * rows : (g + 1) * rows, :]

    def dispatch(g):
        @pl.loop(1, n_dp)
        def _(offset):
            peer = lax.rem(me_d + offset, n_dp)
            pltpu.make_async_remote_copy(
                send.at[peer, pl.ds(g * rows, rows)], recvs[g].at[me_d], send_sem.at[g], move_sem.at[g],
                device_id={"dp": peer}, device_id_type=MESH,
            ).start()

    pack(0)

    @pl.loop(0, n_dp)
    def _(d):
        seg_send[d] = seg[pl.ds(slots[d], 1), :]

    seg_recv[me_d] = seg_send[me_d]
    pl.semaphore_wait(barrier, n_dp + 1)
    dispatch(0)

    @pl.loop(1, n_dp)
    def _(offset):
        peer = lax.rem(me_d + offset, n_dp)
        pltpu.make_async_remote_copy(
            seg_send.at[peer], seg_recv.at[me_d], seg_sem.at[0], seg_sem.at[1],
            device_id={"dp": peer}, device_id_type=MESH,
        ).start()

    for g in range(1, GROUPS):
        pack(g)
        dispatch(g)

    mine = jnp.int32(0)
    for j in range(n_dp):
        mine = mine + jnp.where(dest[j] == me_d, j, 0)
    finish = jnp.int32(0)
    owners = [jnp.int32(0)] * kept
    for i in range(n_dp):
        finish = finish + counts[i]
        owners = [o + jnp.where(finish <= k * n_dp + mine, 1, 0) for k, o in enumerate(owners)]
    for k in range(kept):
        sources[k] = jnp.minimum(owners[k], n_dp - 1)

    gains[...] = gain[...].astype(f32)
    keys[...] = jnp.zeros_like(keys)
    values[...] = jnp.zeros_like(values)

    def ring_copy(z, g, s, way, whole):
        block = ag.at[z, g] if whole else ag.at[z, g, pl.ds(way * half, half)]
        return pltpu.make_async_remote_copy(
            block, block, ring_send.at[way + (0 if whole else 2)], ring_recv.at[way, g, s - 1],
            device_id={"mp": right if way == 0 else left}, device_id_type=MESH,
        )

    def project(z, g, first=False):
        raw = ag[z, g]
        parts, sums = [], None
        for c in range(width // HD):
            x = raw[:, c * HD : (c + 1) * HD].astype(f32)
            parts.append((x * gains[pl.ds(z * (width // HD) + c, 1), :]).astype(bf16))
            sums = x * x if sums is None else sums + x * x
        normed = jnp.concatenate(parts, axis=1)
        at = pl.ds(pl.multiple_of(z * width, width), width)
        queries = jnp.dot(normed, wq[at, :], preferred_element_type=f32)
        pieces = jnp.dot(normed, wkv[at, :], preferred_element_type=f32)
        if first:
            acc[g, :, : 2 * HD] = queries
            acc[g, :, 2 * HD :] = pieces
            squares[g] = sums
        else:
            acc[g, :, : 2 * HD] += queries
            acc[g, :, 2 * HD :] += pieces
            squares[g] += sums

    def open_group(g):
        pltpu.make_async_copy(
            recvs[g].at[pl.ds(0, n_dp - 1)], recvs[g].at[pl.ds(0, n_dp - 1)], move_sem.at[g]
        ).wait()
        for k in range(kept):
            ag[me_z, g, k * rows : (k + 1) * rows, :] = recvs[g][sources[k]]
        for way in range(2):
            ring_copy(me_z, g, 1, way, True).start()
        if g == 0:
            local[2].wait()
            local[3].wait()
        project(me_z, g, first=True)

    def ring_step(g, s):
        from_left = lax.rem(me_z + n_mp - s, n_mp)
        from_right = lax.rem(me_z + s, n_mp)
        for way, z in enumerate((from_left, from_right)):

            @pl.when(s < far)
            def _():
                ring_copy(z, g, s, way, True).wait_recv()

            @pl.when(s == far)
            def _():
                ring_copy(z, g, s, way, False).wait_recv()

            @pl.when(s < far - 1)
            def _():
                ring_copy(z, g, s + 1, way, True).start()

            @pl.when(s == far - 1)
            def _():
                ring_copy(z, g, s + 1, way, False).start()

        project(from_left, g)

        @pl.when(s < far)
        def _():
            project(from_right, g)

    def kv_copy(g):
        return pltpu.make_async_remote_copy(
            kv_mine.at[g], kv_theirs.at[g], kv_send.at[g], kv_recv.at[g],
            device_id={"mp": partner}, device_id_type=MESH,
        )

    def rotated(tensor, g):
        return (
            tensor * tables[g, :, :HD] + pltpu.roll(tensor, HALF, 1) * tables[g, :, HD:]
        ).astype(bf16)

    def close_group(g):
        total = jnp.sum(squares[g], axis=1, keepdims=True)
        scale = lax.rsqrt(total / (n_mp * width) + epsilon)
        kv_mine[g] = (scale * acc[g, :, 2 * HD :]).astype(bf16)
        for h in range(2):
            q_rot[g, h] = rotated(scale * acc[g, :, h * HD : (h + 1) * HD], g)
        kv_copy(g).start()

    def out_copy(g):
        at = pl.ds(pl.multiple_of(g * rows, rows), rows)
        return pltpu.make_async_copy(done.at[g], out.at[:, at], out_sem.at[g])

    def attend(g):
        kv_copy(g).wait_recv()
        own = kv_mine[g].astype(f32)
        other = kv_theirs[g].astype(f32)
        upper = odd == 1
        leading = jnp.where(upper, other, own)
        trailing = jnp.where(upper, own, other)
        low = lax.broadcasted_iota(jnp.int32, own.shape, 1) < HALF
        key_raw = jnp.where(low, leading, pltpu.roll(trailing, HALF, 1))
        value = jnp.where(low, pltpu.roll(leading, HALF, 1), trailing).astype(bf16)
        key = rotated(key_raw, g)
        at = pl.ds(pl.multiple_of(g * rows, rows), rows)
        for k in range(kept):
            part = slice(k * rows, (k + 1) * rows)
            keys[k, at, :] = key[part]
            values[k, at, :] = value[part]
        for k in range(kept):
            part = slice(k * rows, (k + 1) * rows)
            query = jnp.concatenate([q_rot[g, 0, part], q_rot[g, 1, part]], axis=0)
            scores = lax.dot_general(
                query, keys[k], (((1,), (1,)), ((), ())), preferred_element_type=f32
            ) * HD ** (-0.5)
            visible = masks[g, part]
            visible = jnp.concatenate([visible, visible], axis=0)
            scores = jnp.where(visible > 0.5, scores, MASKED)
            weights = jnp.exp(scores - jnp.max(scores, axis=1, keepdims=True))
            shares = (weights / jnp.sum(weights, axis=1, keepdims=True)).astype(bf16)
            mixture = jnp.dot(shares, values[k], preferred_element_type=f32).astype(bf16)
            done[g, k, :, :HD] = mixture[:rows]
            done[g, k, :, HD:] = mixture[rows:]
        out_copy(g).start()

    def prepare():
        pltpu.make_async_copy(
            seg_recv.at[pl.ds(0, n_dp - 1)], seg_recv.at[pl.ds(0, n_dp - 1)], seg_sem.at[1]
        ).wait()
        shape = (block_len, block_len)
        i = lax.broadcasted_iota(jnp.int32, shape, 0)
        j = lax.broadcasted_iota(jnp.int32, shape, 1)
        for k in range(kept):
            across = jnp.broadcast_to(seg_recv[sources[k]].astype(f32), shape)
            same = across == across.T
            position = jnp.sum(jnp.where(same & (j < i), 1.0, 0.0), axis=1, keepdims=True)
            visible = jnp.where(same & (j <= i), 1.0, 0.0)
            chosen = jnp.where(j.astype(f32) == position, 1.0, 0.0)
            turned = jnp.dot(
                chosen, table[...], precision=lax.Precision.HIGHEST, preferred_element_type=f32
            )
            for g in range(GROUPS):
                tables[g, k * rows : (k + 1) * rows, :] = turned[g * rows : (g + 1) * rows]
                masks[g, k * rows : (k + 1) * rows, :] = visible[g * rows : (g + 1) * rows]

    @pl.loop(0, LAG * (GROUPS - 1) + far + 2)
    def _(turn):
        @pl.loop(0, GROUPS)
        def _(g):
            s = turn - LAG * g

            @pl.when((s >= 1) & (s <= far))
            def _():
                ring_step(g, s)

            @pl.when(s == far)
            def _():
                close_group(g)

            @pl.when(s == far + 1)
            def _():
                attend(g)

        for g in range(GROUPS):

            @pl.when(turn == LAG * g)
            def _():
                open_group(g)

        @pl.when(turn == 1)
        def _():
            prepare()

    for g in range(GROUPS):
        moved = send.at[pl.ds(0, n_dp - 1), pl.ds(0, rows)]
        pltpu.make_async_copy(moved, moved, send_sem.at[g]).wait()
        kv_copy(g).wait_send()
        out_copy(g).wait()
    for way in range(2):
        passed = ag.at[pl.ds(0, far - 1)]
        pltpu.make_async_copy(passed, passed, ring_send.at[way]).wait()
        passed = ag.at[0, pl.ds(0, GROUPS), pl.ds(0, half)]
        pltpu.make_async_copy(passed, passed, ring_send.at[way + 2]).wait()
    pltpu.make_async_copy(
        seg_send.at[pl.ds(0, n_dp - 1)], seg_send.at[pl.ds(0, n_dp - 1)], seg_sem.at[0]
    ).wait()


def on_device(n_dp, n_mp, hidden, segments, counts, dest_order, norm_gain, q_weight, kv_weight):
    in_slots, block_len = segments.shape
    width = hidden.shape[1]
    kept = in_slots // 2
    rows = block_len // GROUPS
    group_rows = kept * rows
    depth = q_weight.shape[0]
    vmem, smem = (pl.BlockSpec(memory_space=space) for space in (pltpu.VMEM, pltpu.SMEM))
    anywhere = pl.BlockSpec(memory_space=pl.ANY)
    dma = pltpu.SemaphoreType.DMA
    result = pl.pallas_call(
        functools.partial(kernel, n_dp, n_mp),
        out_shape=jax.ShapeDtypeStruct((kept, block_len, width), bf16),
        in_specs=[anywhere, anywhere, smem, smem, vmem, anywhere, anywhere, vmem],
        out_specs=anywhere,
        scratch_shapes=[
            pltpu.VMEM((in_slots, block_len, width), bf16),
            pltpu.VMEM((in_slots, block_len), jnp.int32),
            pltpu.VMEM((depth, 2 * HD), bf16),
            pltpu.VMEM((depth, HD), bf16),
            pltpu.VMEM((n_dp, block_len, width), bf16),
            pltpu.VMEM((n_dp, 1, block_len), jnp.int32),
            pltpu.VMEM((n_dp, 1, block_len), jnp.int32),
            *[pltpu.VMEM((n_dp, rows, width), bf16)] * GROUPS,
            pltpu.VMEM((n_mp, GROUPS, group_rows, width), bf16),
            pltpu.VMEM((GROUPS, group_rows, 3 * HD), f32),
            pltpu.VMEM((GROUPS, group_rows, HD), f32),
            pltpu.VMEM((GROUPS, group_rows, HD), bf16),
            pltpu.VMEM((GROUPS, group_rows, HD), bf16),
            pltpu.VMEM((GROUPS, 2, group_rows, HD), bf16),
            pltpu.VMEM((kept, block_len, HD), bf16),
            pltpu.VMEM((kept, block_len, HD), bf16),
            pltpu.VMEM((GROUPS, group_rows, 2 * HD), f32),
            pltpu.VMEM((GROUPS, group_rows, HD), f32),
            pltpu.VMEM((n_mp * width // HD, HD), f32),
            pltpu.VMEM((GROUPS, kept, rows, width), bf16),
            pltpu.SMEM((n_dp,), jnp.int32),
            pltpu.SMEM((kept,), jnp.int32),
            dma((4,)),
            dma((GROUPS,)),
            dma((GROUPS,)),
            dma((2,)),
            dma((4,)),
            dma((2, GROUPS, n_mp // 2)),
            dma((GROUPS,)),
            dma((GROUPS,)),
            dma((GROUPS,)),
        ],
        compiler_params=pltpu.CompilerParams(
            collective_id=0, has_side_effects=True, vmem_limit_bytes=60 * 1024 * 1024
        ),
        name="move_gather_attend",
    )(
        hidden.reshape(in_slots, block_len, width),
        segments,
        counts,
        dest_order,
        norm_gain.reshape(n_mp * width // HD, HD),
        q_weight,
        kv_weight,
        jnp.asarray(rope_table(block_len)),
    )
    return result.reshape(kept * block_len, width)


def solution(mesh):
    in_specs = (P("dp", "mp"), P("dp", None), P(), P(), P(), P(None, "mp"), P(None, "mp"))
    return jax.shard_map(
        functools.partial(on_device, mesh.shape["dp"], mesh.shape["mp"]),
        mesh=mesh,
        in_specs=in_specs,
        out_specs=P("dp", "mp"),
        check_vma=False,
    )
```

```python
import functools

import jax
import jax.numpy as jnp
import numpy as np
from jax import lax
from jax.experimental import pallas as pl
from jax.experimental.pallas import tpu as pltpu
from jax.sharding import PartitionSpec as P

HD = 128
HALF = HD // 2
GROUPS = 8
PAIR = 2
READY = 4
epsilon = 1e-05
rope_base = 500000.0
MASKED = -1e30
MESH = pl.DeviceIdType.MESH
f32 = jnp.float32
bf16 = jnp.bfloat16


def rope_table(length):
    frequency = rope_base ** (-(np.arange(HALF, dtype=np.float32) * 2.0) / HD)
    angles = np.arange(length, dtype=np.float32)[:, None] * frequency.astype(np.float32)
    cosine, sine = np.cos(angles), np.sin(angles)
    return np.concatenate([cosine, cosine, -sine, sine], axis=1).astype(np.float32)


def kernel(n_dp, n_mp, hidden, segments, counts, dest, gain, q_weight, kv_weight, table, out, *scratch):
    hid, seg, wq, wkv, send, seg_send, seg_recv, *recvs = scratch[: 7 + GROUPS]
    (
        ag, acc, squares, keys, values, tables, masks, gains, done, slots, sources,
        local_sem, send_sem, move_sem, seg_sem, ring_send, ring_recv, kv_send, kv_recv, out_sem,
    ) = scratch[7 + GROUPS :]
    me_d = lax.axis_index("dp")
    me_z = lax.axis_index("mp")
    in_slots, block_len, width = hid.shape
    kept = in_slots // 2
    rows = block_len // GROUPS
    group_rows = kept * rows
    half = group_rows // 2
    far = n_mp // 2
    right = lax.rem(me_z + 1, n_mp)
    left = lax.rem(me_z + n_mp - 1, n_mp)
    odd = lax.rem(me_z, 2)
    partner = me_z + 1 - 2 * odd
    core = lax.rem(me_d, 2)
    sibling = me_d + 1 - 2 * core
    across = n_dp // 4
    side = lax.rem(me_d // across, 2)
    beside = me_d + across - 2 * across * side
    quarter = kv_weight.shape[0] // 4

    local = [
        pltpu.make_async_copy(hidden, hid, local_sem.at[0]),
        pltpu.make_async_copy(segments, seg, local_sem.at[1]),
        pltpu.make_async_copy(q_weight, wq, local_sem.at[2]),
        pltpu.make_async_copy(kv_weight, wkv.at[:, pl.ds(0, HD)], local_sem.at[3]),
    ]
    for copy in local:
        copy.start()

    barrier = pltpu.get_barrier_semaphore()

    @pl.loop(1, n_dp)
    def _(offset):
        peer = lax.rem(me_d + offset, n_dp)
        pl.semaphore_signal(barrier, inc=1, device_id={"dp": peer}, device_id_type=MESH)

    for neighbour in (left, right):
        pl.semaphore_signal(barrier, inc=1, device_id={"mp": neighbour}, device_id_type=MESH)

    start = jnp.int32(0)
    for i in range(n_dp):
        start = start + jnp.where(i < me_d, counts[i], 0)
    count = counts[me_d]
    wanted = [
        jnp.where(s < count, dest[lax.rem(start + s, n_dp)], -1) for s in range(in_slots)
    ]

    @pl.loop(0, n_dp)
    def _(d):
        slot = jnp.int32(0)
        for s in range(1, in_slots):
            slot = slot + jnp.where(wanted[s] == d, s, 0)
        slots[d] = jnp.minimum(slot, in_slots - 1)

    local[0].wait()
    local[1].wait()

    def pack(g):
        @pl.loop(0, n_dp, unroll=4)
        def _(d):
            send[d, g * rows : (g + 1) * rows, :] = hid[slots[d], g * rows : (g + 1) * rows, :]

        recvs[g][me_d] = send[me_d, g * rows : (g + 1) * rows, :]

    def dispatch(g):
        @pl.loop(1, n_dp)
        def _(offset):
            peer = lax.rem(me_d + offset, n_dp)
            pltpu.make_async_remote_copy(
                send.at[peer, pl.ds(g * rows, rows)], recvs[g].at[me_d], send_sem.at[g], move_sem.at[g],
                device_id={"dp": peer}, device_id_type=MESH,
            ).start()

    pack(0)

    @pl.loop(0, n_dp)
    def _(d):
        seg_send[d] = seg[pl.ds(slots[d], 1), :]

    seg_recv[me_d] = seg_send[me_d]
    pl.semaphore_wait(barrier, n_dp + 1)

    def kv_part(which):
        return pl.ds(pl.multiple_of(which * quarter, quarter), quarter)

    def kv_share(which, stage, device):
        block = wkv.at[kv_part(which), pl.ds(HD, HD)]
        return pltpu.make_async_remote_copy(
            block, block, kv_send.at[stage], kv_recv.at[stage],
            device_id={"dp": device}, device_id_type=MESH,
        )

    own_part = 2 * side + core
    kv_fetch = pltpu.make_async_remote_copy(
        kv_weight.at[kv_part(own_part)], wkv.at[kv_part(own_part), pl.ds(HD, HD)], kv_send.at[0], kv_recv.at[0],
        device_id={"mp": partner}, device_id_type=MESH,
    )
    kv_fetch.start()
    kv_beside = kv_share(own_part, 1, beside)
    kv_sibling = kv_share(own_part, 2, sibling)
    kv_passed = kv_share(2 - 2 * side + core, 3, sibling)

    dispatch(0)

    @pl.loop(1, n_dp)
    def _(offset):
        peer = lax.rem(me_d + offset, n_dp)
        pltpu.make_async_remote_copy(
            seg_send.at[peer], seg_recv.at[me_d], seg_sem.at[0], seg_sem.at[1],
            device_id={"dp": peer}, device_id_type=MESH,
        ).start()

    for g in range(1, GROUPS // 2):
        pack(g)
        dispatch(g)

    mine = jnp.int32(0)
    for j in range(n_dp):
        mine = mine + jnp.where(dest[j] == me_d, j, 0)
    finish = jnp.int32(0)
    owners = [jnp.int32(0)] * kept
    for i in range(n_dp):
        finish = finish + counts[i]
        owners = [o + jnp.where(finish <= k * n_dp + mine, 1, 0) for k, o in enumerate(owners)]
    for k in range(kept):
        sources[k] = jnp.minimum(owners[k], n_dp - 1)

    gains[...] = gain[...].astype(f32)
    keys[...] = jnp.zeros_like(keys)
    values[...] = jnp.zeros_like(values)

    def ring_copy(z, g, s, way, whole):
        block = ag.at[z, g] if whole else ag.at[z, g, pl.ds(way * half, half)]
        return pltpu.make_async_remote_copy(
            block, block, ring_send.at[way + (0 if whole else 2)], ring_recv.at[way, g, s - 1],
            device_id={"mp": right if way == 0 else left}, device_id_type=MESH,
        )

    def project(z, g, first=False):
        raw = ag[z, g]
        parts, sums = [], None
        for c in range(width // HD):
            x = raw[:, c * HD : (c + 1) * HD].astype(f32)
            parts.append((x * gains[pl.ds(z * (width // HD) + c, 1), :]).astype(bf16))
            sums = x * x if sums is None else sums + x * x
        normed = jnp.concatenate(parts, axis=1)
        at = pl.ds(pl.multiple_of(z * width, width), width)
        queries = jnp.dot(normed, wq[at, :], preferred_element_type=f32)
        pieces = jnp.dot(normed, wkv[at, :], preferred_element_type=f32)
        if first:
            acc[g, :, : 2 * HD] = queries
            acc[g, :, 2 * HD :] = pieces
            squares[g] = sums
        else:
            acc[g, :, : 2 * HD] += queries
            acc[g, :, 2 * HD :] += pieces
            squares[g] += sums

    def around(s):
        return lax.rem(me_z + n_mp - s, n_mp), lax.rem(me_z + s, n_mp)

    def open_group(g):
        pltpu.make_async_copy(
            recvs[g].at[pl.ds(0, n_dp - 1)], recvs[g].at[pl.ds(0, n_dp - 1)], move_sem.at[g]
        ).wait()
        for k in range(kept):
            ag[me_z, g, k * rows : (k + 1) * rows, :] = recvs[g][sources[k]]
        for way in range(2):
            ring_copy(me_z, g, 1, way, True).start()

    def ring_step(g, s):
        for way, z in enumerate(around(s)):

            @pl.when(s < far)
            def _():
                ring_copy(z, g, s, way, True).wait_recv()

            @pl.when(s == far)
            def _():
                ring_copy(z, g, s, way, False).wait_recv()

            @pl.when(s < far - 1)
            def _():
                ring_copy(z, g, s + 1, way, True).start()

            @pl.when(s == far - 1)
            def _():
                ring_copy(z, g, s + 1, way, False).start()

    def catch_up(g, s):
        from_left, from_right = around(s)

        @pl.when(s == 0)
        def _():
            project(me_z, g, first=True)

        @pl.when(s > 0)
        def _():
            project(from_left, g)

        @pl.when((s > 0) & (s < far))
        def _():
            project(from_right, g)

    def rotated(tensor, g):
        return (
            tensor * tables[g, :, :HD] + pltpu.roll(tensor, HALF, 1) * tables[g, :, HD:]
        ).astype(bf16)

    def out_copy(g):
        at = pl.ds(pl.multiple_of(g * rows, rows), rows)
        return pltpu.make_async_copy(done.at[g], out.at[:, at], out_sem.at[g])

    def attend(g):
        total = jnp.sum(squares[g], axis=1, keepdims=True)
        scale = lax.rsqrt(total / (n_mp * width) + epsilon)
        query_rows = [rotated(scale * acc[g, :, h * HD : (h + 1) * HD], g) for h in range(2)]
        own = (scale * acc[g, :, 2 * HD : 3 * HD]).astype(bf16).astype(f32)
        other = (scale * acc[g, :, 3 * HD :]).astype(bf16).astype(f32)
        upper = odd == 1
        leading = jnp.where(upper, other, own)
        trailing = jnp.where(upper, own, other)
        low = lax.broadcasted_iota(jnp.int32, own.shape, 1) < HALF
        key_raw = jnp.where(low, leading, pltpu.roll(trailing, HALF, 1))
        value = jnp.where(low, pltpu.roll(leading, HALF, 1), trailing).astype(bf16)
        key = rotated(key_raw, g)
        at = pl.ds(pl.multiple_of(g * rows, rows), rows)
        for k in range(kept):
            part = slice(k * rows, (k + 1) * rows)
            keys[k, at, :] = key[part]
            values[k, at, :] = value[part]
        parts = [slice(k * rows, (k + 1) * rows) for k in range(kept)]
        scores = [
            lax.dot_general(
                jnp.concatenate([query_rows[0][part], query_rows[1][part]], axis=0), keys[k],
                (((1,), (1,)), ((), ())), preferred_element_type=f32,
            )
            for k, part in enumerate(parts)
        ]
        visible = jnp.concatenate([masks[g, part] for part in parts for _ in range(2)], axis=0)
        scores = jnp.where(visible > 0.5, jnp.concatenate(scores, axis=0) * HD ** (-0.5), MASKED)
        weights = jnp.exp(scores - jnp.max(scores, axis=1, keepdims=True))
        shares = (weights * (1.0 / jnp.sum(weights, axis=1, keepdims=True))).astype(bf16)
        mixtures = [
            jnp.dot(shares[2 * k * rows : 2 * (k + 1) * rows], values[k], preferred_element_type=f32)
            for k in range(kept)
        ]
        for k, mixture in enumerate(mixtures):
            done[g, k, :, :HD] = mixture[:rows].astype(bf16)
            done[g, k, :, HD:] = mixture[rows:].astype(bf16)
        out_copy(g).start()

    def prepare():
        pltpu.make_async_copy(
            seg_recv.at[pl.ds(0, n_dp - 1)], seg_recv.at[pl.ds(0, n_dp - 1)], seg_sem.at[1]
        ).wait()
        shape = (block_len, block_len)
        i = lax.broadcasted_iota(jnp.int32, shape, 0)
        j = lax.broadcasted_iota(jnp.int32, shape, 1)
        for k in range(kept):
            across = jnp.broadcast_to(seg_recv[sources[k]].astype(f32), shape)
            same = across == across.T
            position = jnp.sum(jnp.where(same & (j < i), 1.0, 0.0), axis=1, keepdims=True)
            visible = jnp.where(same & (j <= i), 1.0, 0.0)
            chosen = jnp.where(j.astype(f32) == position, 1.0, 0.0)
            turned = jnp.dot(
                chosen, table[...], precision=lax.Precision.HIGHEST, preferred_element_type=f32
            )
            for g in range(GROUPS):
                tables[g, k * rows : (k + 1) * rows, :] = turned[g * rows : (g + 1) * rows]
                masks[g, k * rows : (k + 1) * rows, :] = visible[g * rows : (g + 1) * rows]

    @pl.loop(0, (GROUPS - 1) // PAIR + far + 1)
    def _(turn):
        @pl.when(turn == READY)
        def _():
            local[2].wait()
            local[3].wait()
            kv_sibling.wait_recv()
            kv_passed.wait_recv()

        @pl.loop(0, GROUPS)
        def _(g):
            s = turn - g // PAIR

            @pl.when((s >= 1) & (s <= far))
            def _():
                ring_step(g, s)

            older = turn - READY

            @pl.when((older >= 0) & (older < READY - g // PAIR))
            def _():
                catch_up(g, older)

            @pl.when((turn >= READY) & (s >= 0) & (s <= far))
            def _():
                catch_up(g, s)

            @pl.when(s == far)
            def _():
                attend(g)

        for g in range(GROUPS):

            @pl.when(turn == g // PAIR)
            def _():
                open_group(g)

        @pl.when(turn == 0)
        def _():
            kv_fetch.wait_recv()
            kv_beside.start()
            kv_sibling.start()
            for g in range(GROUPS // 2, GROUPS):
                pack(g)
                dispatch(g)

        @pl.when(turn == 1)
        def _():
            prepare()

        @pl.when(turn == READY - 2)
        def _():
            kv_beside.wait_recv()
            kv_passed.start()

    for g in range(GROUPS):
        moved = send.at[pl.ds(0, n_dp - 1), pl.ds(0, rows)]
        pltpu.make_async_copy(moved, moved, send_sem.at[g]).wait()
        out_copy(g).wait()
    for copy in (kv_fetch, kv_beside, kv_sibling, kv_passed):
        copy.wait_send()
    for way in range(2):
        passed = ag.at[pl.ds(0, far - 1)]
        pltpu.make_async_copy(passed, passed, ring_send.at[way]).wait()
        passed = ag.at[0, pl.ds(0, GROUPS), pl.ds(0, half)]
        pltpu.make_async_copy(passed, passed, ring_send.at[way + 2]).wait()
    pltpu.make_async_copy(
        seg_send.at[pl.ds(0, n_dp - 1)], seg_send.at[pl.ds(0, n_dp - 1)], seg_sem.at[0]
    ).wait()


def on_device(n_dp, n_mp, hidden, segments, counts, dest_order, norm_gain, q_weight, kv_weight):
    in_slots, block_len = segments.shape
    width = hidden.shape[1]
    kept = in_slots // 2
    rows = block_len // GROUPS
    group_rows = kept * rows
    depth = q_weight.shape[0]
    vmem, smem = (pl.BlockSpec(memory_space=space) for space in (pltpu.VMEM, pltpu.SMEM))
    anywhere = pl.BlockSpec(memory_space=pl.ANY)
    dma = pltpu.SemaphoreType.DMA
    result = pl.pallas_call(
        functools.partial(kernel, n_dp, n_mp),
        out_shape=jax.ShapeDtypeStruct((kept, block_len, width), bf16),
        in_specs=[anywhere, anywhere, smem, smem, vmem, anywhere, anywhere, vmem],
        out_specs=anywhere,
        scratch_shapes=[
            pltpu.VMEM((in_slots, block_len, width), bf16),
            pltpu.VMEM((in_slots, block_len), jnp.int32),
            pltpu.VMEM((depth, 2 * HD), bf16),
            pltpu.VMEM((depth, 2 * HD), bf16),
            pltpu.VMEM((n_dp, block_len, width), bf16),
            pltpu.VMEM((n_dp, 1, block_len), jnp.int32),
            pltpu.VMEM((n_dp, 1, block_len), jnp.int32),
            *[pltpu.VMEM((n_dp, rows, width), bf16)] * GROUPS,
            pltpu.VMEM((n_mp, GROUPS, group_rows, width), bf16),
            pltpu.VMEM((GROUPS, group_rows, 4 * HD), f32),
            pltpu.VMEM((GROUPS, group_rows, HD), f32),
            pltpu.VMEM((kept, block_len, HD), bf16),
            pltpu.VMEM((kept, block_len, HD), bf16),
            pltpu.VMEM((GROUPS, group_rows, 2 * HD), f32),
            pltpu.VMEM((GROUPS, group_rows, HD), f32),
            pltpu.VMEM((n_mp * width // HD, HD), f32),
            pltpu.VMEM((GROUPS, kept, rows, width), bf16),
            pltpu.SMEM((n_dp,), jnp.int32),
            pltpu.SMEM((kept,), jnp.int32),
            dma((4,)),
            dma((GROUPS,)),
            dma((GROUPS,)),
            dma((2,)),
            dma((4,)),
            dma((2, GROUPS, n_mp // 2)),
            dma((4,)),
            dma((4,)),
            dma((GROUPS,)),
        ],
        compiler_params=pltpu.CompilerParams(
            collective_id=0, has_side_effects=True, vmem_limit_bytes=60 * 1024 * 1024
        ),
        name="move_gather_attend",
    )(
        hidden.reshape(in_slots, block_len, width),
        segments,
        counts,
        dest_order,
        norm_gain.reshape(n_mp * width // HD, HD),
        q_weight,
        kv_weight,
        jnp.asarray(rope_table(block_len)),
    )
    return result.reshape(kept * block_len, width)


def solution(mesh):
    in_specs = (P("dp", "mp"), P("dp", None), P(), P(), P(), P(None, "mp"), P(None, "mp"))
    return jax.shard_map(
        functools.partial(on_device, mesh.shape["dp"], mesh.shape["mp"]),
        mesh=mesh,
        in_specs=in_specs,
        out_specs=P("dp", "mp"),
        check_vma=False,
    )
```

```python
import functools

import jax
import jax.numpy as jnp
import numpy as np
from jax import lax
from jax.experimental import pallas as pl
from jax.experimental.pallas import tpu as pltpu
from jax.sharding import PartitionSpec as P

HD = 128
HALF = HD // 2
GROUPS = 8
EARLY = 4
READY = 4
epsilon = 1e-05
rope_base = 500000.0
MASKED = -1e30
MESH = pl.DeviceIdType.MESH
f32 = jnp.float32
bf16 = jnp.bfloat16


def rope_table(length):
    frequency = rope_base ** (-(np.arange(HALF, dtype=np.float32) * 2.0) / HD)
    angles = np.arange(length, dtype=np.float32)[:, None] * frequency.astype(np.float32)
    cosine, sine = np.cos(angles), np.sin(angles)
    return np.concatenate([cosine, cosine, -sine, sine], axis=1).astype(np.float32)


def opens(g):
    return g // 2


def kernel(n_dp, n_mp, hidden, segments, counts, dest, gain, q_weight, kv_weight, table, out, *scratch):
    hid, seg, wq, wkv, send, seg_send, seg_recv, *recvs = scratch[: 7 + GROUPS]
    (
        ag, acc, squares, keys, values, tables, masks, gains, slots, sources,
        local_sem, send_sem, move_sem, seg_sem, ring_send, ring_recv, kv_send, kv_recv,
    ) = scratch[7 + GROUPS :]
    me_d = lax.axis_index("dp")
    me_z = lax.axis_index("mp")
    in_slots, block_len, width = hid.shape
    kept = in_slots // 2
    rows = block_len // GROUPS
    group_rows = kept * rows
    half = group_rows // 2
    far = n_mp // 2
    right = lax.rem(me_z + 1, n_mp)
    left = lax.rem(me_z + n_mp - 1, n_mp)
    odd = lax.rem(me_z, 2)
    partner = me_z + 1 - 2 * odd
    core = lax.rem(me_d, 2)
    sibling = me_d + 1 - 2 * core
    across = n_dp // 4
    side = lax.rem(me_d // across, 2)
    beside = me_d + across - 2 * across * side
    quarter = kv_weight.shape[0] // 4

    local = [
        pltpu.make_async_copy(hidden, hid, local_sem.at[0]),
        pltpu.make_async_copy(segments, seg, local_sem.at[1]),
        pltpu.make_async_copy(q_weight, wq, local_sem.at[2]),
        pltpu.make_async_copy(kv_weight, wkv.at[:, pl.ds(0, HD)], local_sem.at[3]),
    ]
    for copy in local:
        copy.start()

    barrier = pltpu.get_barrier_semaphore()

    @pl.loop(1, n_dp)
    def _(offset):
        peer = lax.rem(me_d + offset, n_dp)
        pl.semaphore_signal(barrier, inc=1, device_id={"dp": peer}, device_id_type=MESH)

    for neighbour in (left, right):
        pl.semaphore_signal(barrier, inc=1, device_id={"mp": neighbour}, device_id_type=MESH)

    start = jnp.int32(0)
    for i in range(n_dp):
        start = start + jnp.where(i < me_d, counts[i], 0)
    count = counts[me_d]
    wanted = [
        jnp.where(s < count, dest[lax.rem(start + s, n_dp)], -1) for s in range(in_slots)
    ]

    @pl.loop(0, n_dp)
    def _(d):
        slot = jnp.int32(0)
        for s in range(1, in_slots):
            slot = slot + jnp.where(wanted[s] == d, s, 0)
        slots[d] = jnp.minimum(slot, in_slots - 1)

    local[0].wait()
    local[1].wait()

    def pack(g):
        @pl.loop(0, n_dp, unroll=4)
        def _(d):
            send[d, g * rows : (g + 1) * rows, :] = hid[slots[d], g * rows : (g + 1) * rows, :]

        recvs[g][me_d] = send[me_d, g * rows : (g + 1) * rows, :]

    def dispatch(g):
        @pl.loop(1, n_dp)
        def _(offset):
            peer = lax.rem(me_d + offset, n_dp)
            pltpu.make_async_remote_copy(
                send.at[peer, pl.ds(g * rows, rows)], recvs[g].at[me_d], send_sem.at[g], move_sem.at[g],
                device_id={"dp": peer}, device_id_type=MESH,
            ).start()

    pack(0)

    @pl.loop(0, n_dp)
    def _(d):
        seg_send[d] = seg[pl.ds(slots[d], 1), :]

    seg_recv[me_d] = seg_send[me_d]
    pl.semaphore_wait(barrier, n_dp + 1)

    def kv_part(which):
        return pl.ds(pl.multiple_of(which * quarter, quarter), quarter)

    def kv_share(which, stage, device):
        block = wkv.at[kv_part(which), pl.ds(HD, HD)]
        return pltpu.make_async_remote_copy(
            block, block, kv_send.at[stage], kv_recv.at[stage],
            device_id={"dp": device}, device_id_type=MESH,
        )

    own_part = 2 * side + core
    kv_fetch = pltpu.make_async_remote_copy(
        kv_weight.at[kv_part(own_part)], wkv.at[kv_part(own_part), pl.ds(HD, HD)], kv_send.at[0], kv_recv.at[0],
        device_id={"mp": partner}, device_id_type=MESH,
    )
    kv_fetch.start()
    kv_beside = kv_share(own_part, 1, beside)
    kv_sibling = kv_share(own_part, 2, sibling)
    kv_passed = kv_share(2 - 2 * side + core, 3, sibling)

    dispatch(0)

    @pl.loop(1, n_dp)
    def _(offset):
        peer = lax.rem(me_d + offset, n_dp)
        pltpu.make_async_remote_copy(
            seg_send.at[peer], seg_recv.at[me_d], seg_sem.at[0], seg_sem.at[1],
            device_id={"dp": peer}, device_id_type=MESH,
        ).start()

    for g in range(1, EARLY):
        pack(g)
        dispatch(g)

    mine = jnp.int32(0)
    for j in range(n_dp):
        mine = mine + jnp.where(dest[j] == me_d, j, 0)
    finish = jnp.int32(0)
    owners = [jnp.int32(0)] * kept
    for i in range(n_dp):
        finish = finish + counts[i]
        owners = [o + jnp.where(finish <= k * n_dp + mine, 1, 0) for k, o in enumerate(owners)]
    for k in range(kept):
        sources[k] = jnp.minimum(owners[k], n_dp - 1)

    gains[...] = gain[...].astype(f32)
    keys[...] = jnp.zeros_like(keys)
    values[...] = jnp.zeros_like(values)

    def ring_copy(z, g, s, way, whole):
        block = ag.at[z, g] if whole else ag.at[z, g, pl.ds(way * half, half)]
        return pltpu.make_async_remote_copy(
            block, block, ring_send.at[way + (0 if whole else 2)], ring_recv.at[way, g, s - 1],
            device_id={"mp": right if way == 0 else left}, device_id_type=MESH,
        )

    def project(z, g, first=False):
        raw = ag[z, g]
        parts, sums = [], None
        for c in range(width // HD):
            x = raw[:, c * HD : (c + 1) * HD].astype(f32)
            parts.append((x * gains[pl.ds(z * (width // HD) + c, 1), :]).astype(bf16))
            sums = x * x if sums is None else sums + x * x
        normed = jnp.concatenate(parts, axis=1)
        at = pl.ds(pl.multiple_of(z * width, width), width)
        queries = jnp.dot(normed, wq[at, :], preferred_element_type=f32)
        pieces = jnp.dot(normed, wkv[at, :], preferred_element_type=f32)
        if first:
            acc[g, :, : 2 * HD] = queries
            acc[g, :, 2 * HD :] = pieces
            squares[g] = sums
        else:
            acc[g, :, : 2 * HD] += queries
            acc[g, :, 2 * HD :] += pieces
            squares[g] += sums

    def around(s):
        return lax.rem(me_z + n_mp - s, n_mp), lax.rem(me_z + s, n_mp)

    def open_group(g):
        pltpu.make_async_copy(
            recvs[g].at[pl.ds(0, n_dp - 1)], recvs[g].at[pl.ds(0, n_dp - 1)], move_sem.at[g]
        ).wait()
        for k in range(kept):
            ag[me_z, g, k * rows : (k + 1) * rows, :] = recvs[g][sources[k]]
        for way in range(2):
            ring_copy(me_z, g, 1, way, True).start()
        if opens(g) >= READY:
            project(me_z, g, first=True)

    def ring_step(g, s):
        for way, z in enumerate(around(s)):

            @pl.when(s < far)
            def _():
                ring_copy(z, g, s, way, True).wait_recv()

            @pl.when(s == far)
            def _():
                ring_copy(z, g, s, way, False).wait_recv()

            @pl.when(s < far - 1)
            def _():
                ring_copy(z, g, s + 1, way, True).start()

            @pl.when(s == far - 1)
            def _():
                ring_copy(z, g, s + 1, way, False).start()

    def catch_up(g, s):
        from_left, from_right = around(s)

        @pl.when(s == 0)
        def _():
            project(me_z, g, first=True)

        @pl.when(s > 0)
        def _():
            project(from_left, g)

        @pl.when((s > 0) & (s < far))
        def _():
            project(from_right, g)

    def rotated(tensor, g):
        return (
            tensor * tables[g, :, :HD] + pltpu.roll(tensor, HALF, 1) * tables[g, :, HD:]
        ).astype(bf16)

    def attend(g):
        total = jnp.sum(squares[g], axis=1, keepdims=True)
        scale = lax.rsqrt(total / (n_mp * width) + epsilon)
        query_rows = [rotated(scale * acc[g, :, h * HD : (h + 1) * HD], g) for h in range(2)]
        own = (scale * acc[g, :, 2 * HD : 3 * HD]).astype(bf16).astype(f32)
        other = (scale * acc[g, :, 3 * HD :]).astype(bf16).astype(f32)
        upper = odd == 1
        leading = jnp.where(upper, other, own)
        trailing = jnp.where(upper, own, other)
        low = lax.broadcasted_iota(jnp.int32, own.shape, 1) < HALF
        key_raw = jnp.where(low, leading, pltpu.roll(trailing, HALF, 1))
        value = jnp.where(low, pltpu.roll(leading, HALF, 1), trailing).astype(bf16)
        key = rotated(key_raw, g)
        at = pl.ds(pl.multiple_of(g * rows, rows), rows)
        for k in range(kept):
            part = slice(k * rows, (k + 1) * rows)
            keys[k, at, :] = key[part]
            values[k, at, :] = value[part]
        parts = [slice(k * rows, (k + 1) * rows) for k in range(kept)]
        scores = [
            lax.dot_general(
                jnp.concatenate([query_rows[0][part], query_rows[1][part]], axis=0), keys[k],
                (((1,), (1,)), ((), ())), preferred_element_type=f32,
            )
            for k, part in enumerate(parts)
        ]
        visible = jnp.concatenate([masks[g, part] for part in parts for _ in range(2)], axis=0)
        scores = jnp.where(visible > 0.5, jnp.concatenate(scores, axis=0) * HD ** (-0.5), MASKED)
        weights = jnp.exp(scores - jnp.max(scores, axis=1, keepdims=True))
        shares = (weights * (1.0 / jnp.sum(weights, axis=1, keepdims=True))).astype(bf16)
        mixtures = [
            jnp.dot(shares[2 * k * rows : 2 * (k + 1) * rows], values[k], preferred_element_type=f32)
            for k in range(kept)
        ]
        for k, mixture in enumerate(mixtures):
            out[k, at, :HD] = mixture[:rows].astype(bf16)
            out[k, at, HD:] = mixture[rows:].astype(bf16)

    def prepare():
        pltpu.make_async_copy(
            seg_recv.at[pl.ds(0, n_dp - 1)], seg_recv.at[pl.ds(0, n_dp - 1)], seg_sem.at[1]
        ).wait()
        shape = (block_len, block_len)
        i = lax.broadcasted_iota(jnp.int32, shape, 0)
        j = lax.broadcasted_iota(jnp.int32, shape, 1)
        for k in range(kept):
            across = jnp.broadcast_to(seg_recv[sources[k]].astype(f32), shape)
            same = across == across.T
            position = jnp.sum(jnp.where(same & (j < i), 1.0, 0.0), axis=1, keepdims=True)
            visible = jnp.where(same & (j <= i), 1.0, 0.0)
            chosen = jnp.where(j.astype(f32) == position, 1.0, 0.0)
            turned = jnp.dot(
                chosen, table[...], precision=lax.Precision.HIGHEST, preferred_element_type=f32
            )
            for g in range(GROUPS):
                tables[g, k * rows : (k + 1) * rows, :] = turned[g * rows : (g + 1) * rows]
                masks[g, k * rows : (k + 1) * rows, :] = visible[g * rows : (g + 1) * rows]

    @pl.loop(0, opens(GROUPS - 1) + far + 1)
    def _(turn):
        @pl.when(turn == READY)
        def _():
            local[2].wait()
            local[3].wait()
            kv_sibling.wait_recv()
            kv_passed.wait_recv()

        @pl.loop(0, GROUPS)
        def _(g):
            s = turn - opens(g)

            @pl.when((s >= 1) & (s <= far))
            def _():
                ring_step(g, s)

            older = turn - READY

            @pl.when((older >= 0) & (older < READY - opens(g)))
            def _():
                catch_up(g, older)

            @pl.when((turn >= READY) & (s >= 1) & (s <= far))
            def _():
                catch_up(g, s)

            @pl.when(s == far)
            def _():
                attend(g)

        for g in range(GROUPS):

            @pl.when(turn == opens(g))
            def _():
                open_group(g)

        @pl.when(turn == 0)
        def _():
            kv_fetch.wait_recv()
            kv_beside.start()
            kv_sibling.start()
            for g in range(EARLY, GROUPS):
                pack(g)
                dispatch(g)

        @pl.when(turn == 1)
        def _():
            prepare()

        @pl.when(turn == READY - 2)
        def _():
            kv_beside.wait_recv()
            kv_passed.start()

    for g in range(GROUPS):
        moved = send.at[pl.ds(0, n_dp - 1), pl.ds(0, rows)]
        pltpu.make_async_copy(moved, moved, send_sem.at[g]).wait()
    for copy in (kv_fetch, kv_beside, kv_sibling, kv_passed):
        copy.wait_send()
    for way in range(2):
        passed = ag.at[pl.ds(0, far - 1)]
        pltpu.make_async_copy(passed, passed, ring_send.at[way]).wait()
        passed = ag.at[0, pl.ds(0, GROUPS), pl.ds(0, half)]
        pltpu.make_async_copy(passed, passed, ring_send.at[way + 2]).wait()
    pltpu.make_async_copy(
        seg_send.at[pl.ds(0, n_dp - 1)], seg_send.at[pl.ds(0, n_dp - 1)], seg_sem.at[0]
    ).wait()


def on_device(n_dp, n_mp, hidden, segments, counts, dest_order, norm_gain, q_weight, kv_weight):
    in_slots, block_len = segments.shape
    width = hidden.shape[1]
    kept = in_slots // 2
    rows = block_len // GROUPS
    group_rows = kept * rows
    depth = q_weight.shape[0]
    vmem, smem = (pl.BlockSpec(memory_space=space) for space in (pltpu.VMEM, pltpu.SMEM))
    anywhere = pl.BlockSpec(memory_space=pl.ANY)
    dma = pltpu.SemaphoreType.DMA
    result = pl.pallas_call(
        functools.partial(kernel, n_dp, n_mp),
        out_shape=pltpu.VMEM((kept, block_len, width), bf16),
        in_specs=[anywhere, anywhere, smem, smem, vmem, anywhere, anywhere, vmem],
        out_specs=vmem,
        scratch_shapes=[
            pltpu.VMEM((in_slots, block_len, width), bf16),
            pltpu.VMEM((in_slots, block_len), jnp.int32),
            pltpu.VMEM((depth, 2 * HD), bf16),
            pltpu.VMEM((depth, 2 * HD), bf16),
            pltpu.VMEM((n_dp, block_len, width), bf16),
            pltpu.VMEM((n_dp, 1, block_len), jnp.int32),
            pltpu.VMEM((n_dp, 1, block_len), jnp.int32),
            *[pltpu.VMEM((n_dp, rows, width), bf16)] * GROUPS,
            pltpu.VMEM((n_mp, GROUPS, group_rows, width), bf16),
            pltpu.VMEM((GROUPS, group_rows, 4 * HD), f32),
            pltpu.VMEM((GROUPS, group_rows, HD), f32),
            pltpu.VMEM((kept, block_len, HD), bf16),
            pltpu.VMEM((kept, block_len, HD), bf16),
            pltpu.VMEM((GROUPS, group_rows, 2 * HD), f32),
            pltpu.VMEM((GROUPS, group_rows, HD), f32),
            pltpu.VMEM((n_mp * width // HD, HD), f32),
            pltpu.SMEM((n_dp,), jnp.int32),
            pltpu.SMEM((kept,), jnp.int32),
            dma((4,)),
            dma((GROUPS,)),
            dma((GROUPS,)),
            dma((2,)),
            dma((4,)),
            dma((2, GROUPS, n_mp // 2)),
            dma((4,)),
            dma((4,)),
        ],
        compiler_params=pltpu.CompilerParams(
            collective_id=0, has_side_effects=True, vmem_limit_bytes=60 * 1024 * 1024
        ),
        name="move_gather_attend",
    )(
        hidden.reshape(in_slots, block_len, width),
        segments,
        counts,
        dest_order,
        norm_gain.reshape(n_mp * width // HD, HD),
        q_weight,
        kv_weight,
        jnp.asarray(rope_table(block_len)),
    )
    return result.reshape(kept * block_len, width)


def solution(mesh):
    in_specs = (P("dp", "mp"), P("dp", None), P(), P(), P(), P(None, "mp"), P(None, "mp"))
    return jax.shard_map(
        functools.partial(on_device, mesh.shape["dp"], mesh.shape["mp"]),
        mesh=mesh,
        in_specs=in_specs,
        out_specs=P("dp", "mp"),
        check_vma=False,
    )
```

```python
import functools

import jax
import jax.numpy as jnp
import numpy as np
from jax import lax
from jax.experimental import pallas as pl
from jax.experimental.pallas import tpu as pltpu
from jax.sharding import PartitionSpec as P

HD = 128
HALF = HD // 2
GROUPS = 8
EARLY = 4
READY = 4
epsilon = 1e-05
rope_base = 500000.0
MASKED = -1e30
MESH = pl.DeviceIdType.MESH
f32 = jnp.float32
bf16 = jnp.bfloat16


def rope_table(length):
    frequency = rope_base ** (-(np.arange(HALF, dtype=np.float32) * 2.0) / HD)
    angles = np.arange(length, dtype=np.float32)[:, None] * frequency.astype(np.float32)
    cosine, sine = np.cos(angles), np.sin(angles)
    return np.concatenate([cosine, cosine, -sine, sine], axis=1).astype(np.float32)


def opens(g):
    return g // 2


def kernel(n_dp, n_mp, hidden, segments, counts, dest, gain_in, q_weight, kv_weight, table_in, out, *scratch):
    hid, seg, wq, wkv, send, seg_send, seg_recv, *recvs = scratch[: 7 + GROUPS]
    (
        ag, acc, squares, keys, values, tables, masks, gains, gain, table, slots, sources,
        local_sem, send_sem, move_sem, seg_sem, ring_send, ring_recv, kv_send, kv_recv,
    ) = scratch[7 + GROUPS :]
    me_d = lax.axis_index("dp")
    me_z = lax.axis_index("mp")
    in_slots, block_len, width = hid.shape
    kept = in_slots // 2
    rows = block_len // GROUPS
    group_rows = kept * rows
    half = group_rows // 2
    far = n_mp // 2
    right = lax.rem(me_z + 1, n_mp)
    left = lax.rem(me_z + n_mp - 1, n_mp)
    odd = lax.rem(me_z, 2)
    partner = me_z + 1 - 2 * odd
    core = lax.rem(me_d, 2)
    sibling = me_d + 1 - 2 * core
    across = n_dp // 4
    side = lax.rem(me_d // across, 2)
    beside = me_d + across - 2 * across * side
    quarter = kv_weight.shape[0] // 4

    local = [
        pltpu.make_async_copy(hidden, hid, local_sem.at[0]),
        pltpu.make_async_copy(segments, seg, local_sem.at[1]),
        pltpu.make_async_copy(q_weight, wq, local_sem.at[2]),
        pltpu.make_async_copy(kv_weight, wkv.at[:, pl.ds(0, HD)], local_sem.at[3]),
        pltpu.make_async_copy(gain_in, gain, local_sem.at[4]),
        pltpu.make_async_copy(table_in, table, local_sem.at[5]),
    ]
    for copy in local:
        copy.start()

    barrier = pltpu.get_barrier_semaphore()
    for neighbour in (left, right):
        pl.semaphore_signal(barrier, inc=1, device_id={"mp": neighbour}, device_id_type=MESH)

    @pl.loop(1, n_dp)
    def _(offset):
        peer = lax.rem(me_d + offset, n_dp)
        pl.semaphore_signal(barrier, inc=1, device_id={"dp": peer}, device_id_type=MESH)

    start = jnp.int32(0)
    for i in range(n_dp):
        start = start + jnp.where(i < me_d, counts[i], 0)
    count = counts[me_d]
    wanted = [
        jnp.where(s < count, dest[lax.rem(start + s, n_dp)], -1) for s in range(in_slots)
    ]

    @pl.loop(0, n_dp)
    def _(d):
        slot = jnp.int32(0)
        for s in range(1, in_slots):
            slot = slot + jnp.where(wanted[s] == d, s, 0)
        slots[d] = jnp.minimum(slot, in_slots - 1)

    local[0].wait()
    local[1].wait()

    def pack(g):
        @pl.loop(0, n_dp, unroll=4)
        def _(d):
            send[d, g * rows : (g + 1) * rows, :] = hid[slots[d], g * rows : (g + 1) * rows, :]

        recvs[g][me_d] = send[me_d, g * rows : (g + 1) * rows, :]

    def dispatch(g):
        @pl.loop(1, n_dp)
        def _(offset):
            peer = lax.rem(me_d + offset, n_dp)
            pltpu.make_async_remote_copy(
                send.at[peer, pl.ds(g * rows, rows)], recvs[g].at[me_d], send_sem.at[g], move_sem.at[g],
                device_id={"dp": peer}, device_id_type=MESH,
            ).start()

    pack(0)

    @pl.loop(0, n_dp)
    def _(d):
        seg_send[d] = seg[pl.ds(slots[d], 1), :]

    seg_recv[me_d] = seg_send[me_d]
    pl.semaphore_wait(barrier, n_dp + 1)

    def kv_part(which):
        return pl.ds(pl.multiple_of(which * quarter, quarter), quarter)

    def kv_share(which, stage, device):
        block = wkv.at[kv_part(which), pl.ds(HD, HD)]
        return pltpu.make_async_remote_copy(
            block, block, kv_send.at[stage], kv_recv.at[stage],
            device_id={"dp": device}, device_id_type=MESH,
        )

    own_part = 2 * side + core
    kv_fetch = pltpu.make_async_remote_copy(
        kv_weight.at[kv_part(own_part)], wkv.at[kv_part(own_part), pl.ds(HD, HD)], kv_send.at[0], kv_recv.at[0],
        device_id={"mp": partner}, device_id_type=MESH,
    )
    kv_fetch.start()
    kv_beside = kv_share(own_part, 1, beside)
    kv_sibling = kv_share(own_part, 2, sibling)
    kv_passed = kv_share(2 - 2 * side + core, 3, sibling)

    dispatch(0)

    @pl.loop(1, n_dp)
    def _(offset):
        peer = lax.rem(me_d + offset, n_dp)
        pltpu.make_async_remote_copy(
            seg_send.at[peer], seg_recv.at[me_d], seg_sem.at[0], seg_sem.at[1],
            device_id={"dp": peer}, device_id_type=MESH,
        ).start()

    for g in range(1, EARLY):
        pack(g)
        dispatch(g)

    mine = jnp.int32(0)
    for j in range(n_dp):
        mine = mine + jnp.where(dest[j] == me_d, j, 0)
    finish = jnp.int32(0)
    owners = [jnp.int32(0)] * kept
    for i in range(n_dp):
        finish = finish + counts[i]
        owners = [o + jnp.where(finish <= k * n_dp + mine, 1, 0) for k, o in enumerate(owners)]
    for k in range(kept):
        sources[k] = jnp.minimum(owners[k], n_dp - 1)

    local[4].wait()
    gains[...] = gain[...].astype(f32)
    keys[...] = jnp.zeros_like(keys)
    values[...] = jnp.zeros_like(values)

    def ring_copy(z, g, s, way, whole):
        block = ag.at[z, g] if whole else ag.at[z, g, pl.ds(way * half, half)]
        return pltpu.make_async_remote_copy(
            block, block, ring_send.at[way + (0 if whole else 2)], ring_recv.at[way, g, s - 1],
            device_id={"mp": right if way == 0 else left}, device_id_type=MESH,
        )

    def project(z, g, first=False):
        raw = ag[z, g]
        parts, sums = [], None
        for c in range(width // HD):
            x = raw[:, c * HD : (c + 1) * HD].astype(f32)
            parts.append((x * gains[pl.ds(z * (width // HD) + c, 1), :]).astype(bf16))
            sums = x * x if sums is None else sums + x * x
        normed = jnp.concatenate(parts, axis=1)
        at = pl.ds(pl.multiple_of(z * width, width), width)
        queries = jnp.dot(normed, wq[at, :], preferred_element_type=f32)
        pieces = jnp.dot(normed, wkv[at, :], preferred_element_type=f32)
        if first:
            acc[g, :, : 2 * HD] = queries
            acc[g, :, 2 * HD :] = pieces
            squares[g] = sums
        else:
            acc[g, :, : 2 * HD] += queries
            acc[g, :, 2 * HD :] += pieces
            squares[g] += sums

    def around(s):
        return lax.rem(me_z + n_mp - s, n_mp), lax.rem(me_z + s, n_mp)

    def open_group(g):
        pltpu.make_async_copy(
            recvs[g].at[pl.ds(0, n_dp - 1)], recvs[g].at[pl.ds(0, n_dp - 1)], move_sem.at[g]
        ).wait()
        for k in range(kept):
            ag[me_z, g, k * rows : (k + 1) * rows, :] = recvs[g][sources[k]]
        for way in range(2):
            ring_copy(me_z, g, 1, way, True).start()
        if opens(g) >= READY:
            project(me_z, g, first=True)

    def ring_step(g, s):
        for way, z in enumerate(around(s)):

            @pl.when(s < far)
            def _():
                ring_copy(z, g, s, way, True).wait_recv()

            @pl.when(s == far)
            def _():
                ring_copy(z, g, s, way, False).wait_recv()

            @pl.when(s < far - 1)
            def _():
                ring_copy(z, g, s + 1, way, True).start()

            @pl.when(s == far - 1)
            def _():
                ring_copy(z, g, s + 1, way, False).start()

    def catch_up(g, s):
        from_left, from_right = around(s)

        @pl.when(s == 0)
        def _():
            project(me_z, g, first=True)

        @pl.when(s > 0)
        def _():
            project(from_left, g)

        @pl.when((s > 0) & (s < far))
        def _():
            project(from_right, g)

    def rotated(tensor, g):
        return (
            tensor * tables[g, :, :HD] + pltpu.roll(tensor, HALF, 1) * tables[g, :, HD:]
        ).astype(bf16)

    def attend(g):
        total = jnp.sum(squares[g], axis=1, keepdims=True)
        scale = lax.rsqrt(total / (n_mp * width) + epsilon)
        query_rows = [rotated(scale * acc[g, :, h * HD : (h + 1) * HD], g) for h in range(2)]
        own = (scale * acc[g, :, 2 * HD : 3 * HD]).astype(bf16).astype(f32)
        other = (scale * acc[g, :, 3 * HD :]).astype(bf16).astype(f32)
        upper = odd == 1
        leading = jnp.where(upper, other, own)
        trailing = jnp.where(upper, own, other)
        low = lax.broadcasted_iota(jnp.int32, own.shape, 1) < HALF
        key_raw = jnp.where(low, leading, pltpu.roll(trailing, HALF, 1))
        value = jnp.where(low, pltpu.roll(leading, HALF, 1), trailing).astype(bf16)
        key = rotated(key_raw, g)
        at = pl.ds(pl.multiple_of(g * rows, rows), rows)
        for k in range(kept):
            part = slice(k * rows, (k + 1) * rows)
            keys[k, at, :] = key[part]
            values[k, at, :] = value[part]
        parts = [slice(k * rows, (k + 1) * rows) for k in range(kept)]
        scores = [
            lax.dot_general(
                jnp.concatenate([query_rows[0][part], query_rows[1][part]], axis=0), keys[k],
                (((1,), (1,)), ((), ())), preferred_element_type=f32,
            )
            for k, part in enumerate(parts)
        ]
        visible = jnp.concatenate([masks[g, part] for part in parts for _ in range(2)], axis=0)
        scores = jnp.where(visible > 0.5, jnp.concatenate(scores, axis=0) * HD ** (-0.5), MASKED)
        weights = jnp.exp(scores - jnp.max(scores, axis=1, keepdims=True))
        shares = (weights * (1.0 / jnp.sum(weights, axis=1, keepdims=True))).astype(bf16)
        mixtures = [
            jnp.dot(shares[2 * k * rows : 2 * (k + 1) * rows], values[k], preferred_element_type=f32)
            for k in range(kept)
        ]
        for k, mixture in enumerate(mixtures):
            out[k, at, :HD] = mixture[:rows].astype(bf16)
            out[k, at, HD:] = mixture[rows:].astype(bf16)

    def prepare():
        local[5].wait()
        pltpu.make_async_copy(
            seg_recv.at[pl.ds(0, n_dp - 1)], seg_recv.at[pl.ds(0, n_dp - 1)], seg_sem.at[1]
        ).wait()
        shape = (block_len, block_len)
        i = lax.broadcasted_iota(jnp.int32, shape, 0)
        j = lax.broadcasted_iota(jnp.int32, shape, 1)
        for k in range(kept):
            across = jnp.broadcast_to(seg_recv[sources[k]].astype(f32), shape)
            same = across == across.T
            position = jnp.sum(jnp.where(same & (j < i), 1.0, 0.0), axis=1, keepdims=True)
            visible = jnp.where(same & (j <= i), 1.0, 0.0)
            chosen = jnp.where(j.astype(f32) == position, 1.0, 0.0)
            turned = jnp.dot(
                chosen, table[...], precision=lax.Precision.HIGHEST, preferred_element_type=f32
            )
            for g in range(GROUPS):
                tables[g, k * rows : (k + 1) * rows, :] = turned[g * rows : (g + 1) * rows]
                masks[g, k * rows : (k + 1) * rows, :] = visible[g * rows : (g + 1) * rows]

    @pl.loop(0, opens(GROUPS - 1) + far + 1)
    def _(turn):
        @pl.when(turn == READY)
        def _():
            local[2].wait()
            local[3].wait()
            kv_sibling.wait_recv()
            kv_passed.wait_recv()

        @pl.loop(0, GROUPS)
        def _(g):
            s = turn - opens(g)

            @pl.when((s >= 1) & (s <= far))
            def _():
                ring_step(g, s)

            older = turn - READY

            @pl.when((older >= 0) & (older < READY - opens(g)))
            def _():
                catch_up(g, older)

            @pl.when((turn >= READY) & (s >= 1) & (s <= far))
            def _():
                catch_up(g, s)

            @pl.when(s == far)
            def _():
                attend(g)

        for g in range(GROUPS):

            @pl.when(turn == opens(g))
            def _():
                open_group(g)

        @pl.when(turn == 0)
        def _():
            kv_fetch.wait_recv()
            kv_beside.start()
            kv_sibling.start()
            for g in range(EARLY, GROUPS):
                pack(g)
                dispatch(g)

        @pl.when(turn == 1)
        def _():
            prepare()

        @pl.when(turn == READY - 2)
        def _():
            kv_beside.wait_recv()
            kv_passed.start()

    for g in range(GROUPS):
        moved = send.at[pl.ds(0, n_dp - 1), pl.ds(0, rows)]
        pltpu.make_async_copy(moved, moved, send_sem.at[g]).wait()
    for copy in (kv_fetch, kv_beside, kv_sibling, kv_passed):
        copy.wait_send()
    for way in range(2):
        passed = ag.at[pl.ds(0, far - 1)]
        pltpu.make_async_copy(passed, passed, ring_send.at[way]).wait()
        passed = ag.at[0, pl.ds(0, GROUPS), pl.ds(0, half)]
        pltpu.make_async_copy(passed, passed, ring_send.at[way + 2]).wait()
    pltpu.make_async_copy(
        seg_send.at[pl.ds(0, n_dp - 1)], seg_send.at[pl.ds(0, n_dp - 1)], seg_sem.at[0]
    ).wait()


def on_device(n_dp, n_mp, hidden, segments, counts, dest_order, norm_gain, q_weight, kv_weight):
    in_slots, block_len = segments.shape
    width = hidden.shape[1]
    kept = in_slots // 2
    rows = block_len // GROUPS
    group_rows = kept * rows
    depth = q_weight.shape[0]
    vmem, smem = (pl.BlockSpec(memory_space=space) for space in (pltpu.VMEM, pltpu.SMEM))
    anywhere = pl.BlockSpec(memory_space=pl.ANY)
    dma = pltpu.SemaphoreType.DMA
    result = pl.pallas_call(
        functools.partial(kernel, n_dp, n_mp),
        out_shape=pltpu.VMEM((kept, block_len, width), bf16),
        in_specs=[anywhere, anywhere, smem, smem, anywhere, anywhere, anywhere, anywhere],
        out_specs=vmem,
        scratch_shapes=[
            pltpu.VMEM((in_slots, block_len, width), bf16),
            pltpu.VMEM((in_slots, block_len), jnp.int32),
            pltpu.VMEM((depth, 2 * HD), bf16),
            pltpu.VMEM((depth, 2 * HD), bf16),
            pltpu.VMEM((n_dp, block_len, width), bf16),
            pltpu.VMEM((n_dp, 1, block_len), jnp.int32),
            pltpu.VMEM((n_dp, 1, block_len), jnp.int32),
            *[pltpu.VMEM((n_dp, rows, width), bf16)] * GROUPS,
            pltpu.VMEM((n_mp, GROUPS, group_rows, width), bf16),
            pltpu.VMEM((GROUPS, group_rows, 4 * HD), f32),
            pltpu.VMEM((GROUPS, group_rows, HD), f32),
            pltpu.VMEM((kept, block_len, HD), bf16),
            pltpu.VMEM((kept, block_len, HD), bf16),
            pltpu.VMEM((GROUPS, group_rows, 2 * HD), f32),
            pltpu.VMEM((GROUPS, group_rows, HD), f32),
            pltpu.VMEM((n_mp * width // HD, HD), f32),
            pltpu.VMEM((n_mp * width // HD, HD), bf16),
            pltpu.VMEM((block_len, 2 * HD), f32),
            pltpu.SMEM((n_dp,), jnp.int32),
            pltpu.SMEM((kept,), jnp.int32),
            dma((6,)),
            dma((GROUPS,)),
            dma((GROUPS,)),
            dma((2,)),
            dma((4,)),
            dma((2, GROUPS, n_mp // 2)),
            dma((4,)),
            dma((4,)),
        ],
        compiler_params=pltpu.CompilerParams(
            collective_id=0, has_side_effects=True, vmem_limit_bytes=60 * 1024 * 1024
        ),
        name="move_gather_attend",
    )(
        hidden.reshape(in_slots, block_len, width),
        segments,
        counts,
        dest_order,
        norm_gain.reshape(n_mp * width // HD, HD),
        q_weight,
        kv_weight,
        jnp.asarray(rope_table(block_len)),
    )
    return result.reshape(kept * block_len, width)


def solution(mesh):
    in_specs = (P("dp", "mp"), P("dp", None), P(), P(), P(), P(None, "mp"), P(None, "mp"))
    return jax.shard_map(
        functools.partial(on_device, mesh.shape["dp"], mesh.shape["mp"]),
        mesh=mesh,
        in_specs=in_specs,
        out_specs=P("dp", "mp"),
        check_vma=False,
    )
```
